32 devices in a mesh: cells: 16 (over z, y, x), genes: 2 (over core).
Axes of the slice: x: 2, y: 2, z: 4, core: 2. Of those that a mesh axis runs over, the one named last changes fastest.
Arguments:
- expression: bfloat16 [16384, 4096], P('cells', 'genes'), may hold values from 0 to 3
- loading: bfloat16 [4096, 128], P('genes'), may hold values from -0.09375 to 0.09375
- kernel_width: bfloat16 [16384], P(('cells', 'genes')), may hold values from 10 to 20
- cluster: int32 [16384, 1], P(('cells', 'genes')), may hold values from 0 to 31, as said below
- quality: int32 [16384], P(('cells', 'genes')), may hold values from 0 to 1, as said below
Outputs:
- smoothed: float32 [16384, 128], P(('cells', 'genes'))
The draws below stay inside these ranges and needn't reach their ends.
Inputs may be any that keep to these rules, and one draw needn't show every extreme that they name: Among the 512 cells of one device no cluster appears more than 32 times; one cluster appears exactly 32 times in every device, so that it holds 1024 cells; every cluster appears somewhere. All cells of a cluster that holds 1024 cells have quality 1.
All inputs are finite; a program needn't handle non-finite values.
Results may differ from the reference program's by a relative error of at most 0.0029.
Values may be sent and summed in bfloat16 or wider, within the bound.
No kernel may reach another device: no remote copies, remote signals or barrier semaphores. Data moves between devices by JAX's collectives and lax.ppermute only.
A program may use at most 64 MiB of HBM per device.

```python
import math
import jax
import jax.numpy as jnp
from jax import lax

G = 4096
K = 128
ROWS_DEV = 512
CAP = 32
SLOTS = 1024
CLUSTERS = 32
CELLS = 16384
DEVICES = 32


def labels_and_hot(key):
    hot = jax.random.randint(jax.random.fold_in(key, 1), (), 0, CLUSTERS).astype(jnp.int32)
    others = jax.random.permutation(jax.random.fold_in(key, 2), CLUSTERS - 1).astype(jnp.int32)
    row_ids = jnp.arange(ROWS_DEV, dtype=jnp.int32)
    device_ids = jnp.arange(DEVICES, dtype=jnp.int32)
    ranked = device_ids[:, None] * (ROWS_DEV - CAP) + jnp.maximum(row_ids[None, :] - CAP, 0)
    picked = others[ranked % (CLUSTERS - 1)]
    other_ids = picked + (picked >= hot).astype(jnp.int32)
    base = jnp.where(row_ids[None, :] < CAP, hot, other_ids).astype(jnp.int32)
    device_keys = jax.random.split(jax.random.fold_in(key, 3), DEVICES)
    orders = jax.vmap(lambda one_key: jax.random.permutation(one_key, ROWS_DEV))(device_keys).astype(jnp.int32)
    labels = jnp.take_along_axis(base, orders, axis=1).reshape(DEVICES * ROWS_DEV).astype(jnp.int32)
    return (labels, hot)


def draw_cluster(key, part):
    labels, hot = labels_and_hot(key)
    return labels[:, None].astype(jnp.int32)


def draw_quality(key, part):
    labels, hot = labels_and_hot(key)
    rolls = jax.random.randint(jax.random.fold_in(key, 7), (DEVICES * ROWS_DEV,), 0, 5)
    passed = (rolls < 4) | (labels == hot)
    return passed.astype(jnp.int32)


def level_of(key, extent, cuts, least, high):
    loudness = 1.0
    for axis_at, parts in cuts:
        draws = jax.random.uniform(jax.random.fold_in(jax.random.fold_in(key, 6), axis_at), (parts,), jnp.float32, least / len(cuts), high / len(cuts))
        loudness = loudness * jnp.repeat(jnp.exp(draws), extent[axis_at] // parts).reshape((-1,) + (1,) * (len(extent) - 1 - axis_at))
    return loudness


def scatter_about(own_key, dims, deviation, limit, pieces=(), kind=jnp.bfloat16):
    drawn = jax.random.normal(own_key, dims, jnp.float32) * deviation
    if len(pieces) > 0:
        drawn = level_of(own_key, dims, pieces, -0.22, 0.18) * drawn
    return jnp.clip(drawn, min=-limit, max=limit).astype(kind)


def setup_inputs(seed: int = 0) -> dict:
    key_list = jax.random.split(jax.random.key(seed), 6)
    expression = jnp.clip(3.0 * jax.random.uniform(key_list[0], (CELLS, G), jnp.float32) ** level_of(key_list[0], (CELLS, G), ((0, 16), (1, 2)), -0.2, 0.2), 0.0, 3.0).astype(jnp.bfloat16)
    loading = scatter_about(key_list[1], (G, K), G ** -0.5, 0.09375, ((0, 2),))
    kernel_width = jnp.clip(jnp.exp(math.log(20.0) - 0.6931472 * jax.random.uniform(key_list[2], (CELLS,), jnp.float32) ** level_of(key_list[2], (CELLS,), ((0, 32),), -0.2, 0.2)), 10.0, 20.0).astype(jnp.bfloat16)
    cluster = draw_cluster(jax.random.fold_in(key_list[5], 71), 0)
    quality = draw_quality(jax.random.fold_in(key_list[5], 71), 0)
    return dict(expression=expression, loading=loading, kernel_width=kernel_width, cluster=cluster, quality=quality)


def diffuse(slot_rows, widths):
    widths = widths.astype(jnp.float32)
    present = (widths > 0).astype(jnp.float32)
    as_float = slot_rows.astype(jnp.float32)
    sq_norms = jnp.sum(as_float * as_float, axis=1)
    products = jnp.dot(slot_rows, slot_rows.T, preferred_element_type=jnp.float32)
    distance = sq_norms[:, None] + sq_norms[None, :] - 2.0 * products
    pair_live = present[:, None] * present[None, :]
    width_pair = jnp.where(pair_live > 0, widths[:, None] * widths[None, :], jnp.ones_like(pair_live))
    affinity = jnp.exp(-distance / width_pair) * pair_live
    row_total = jnp.sum(affinity, axis=1) + (1.0 - present)
    weights = (affinity / row_total[:, None]).astype(jnp.bfloat16)
    one_step = 0.5 * (as_float + jnp.dot(weights, slot_rows, preferred_element_type=jnp.float32))
    two_steps = 0.5 * (one_step + jnp.dot(weights, one_step.astype(jnp.bfloat16), preferred_element_type=jnp.float32))
    return two_steps


def reference(expression, loading, kernel_width, cluster, quality):
    embedded = jnp.dot(expression, loading, preferred_element_type=jnp.float32).astype(jnp.bfloat16)
    labels = cluster[:, 0].astype(jnp.int32)
    is_live = quality == 1
    keyed_ids = jnp.where(is_live, labels, CLUSTERS).astype(jnp.int32)
    sort_order = jnp.argsort(keyed_ids, stable=True).astype(jnp.int32)
    counts = jax.ops.segment_sum(jnp.ones_like(keyed_ids), keyed_ids, num_segments=CLUSTERS + 1).astype(jnp.int32)
    starts = (jnp.cumsum(counts) - counts).astype(jnp.int32)
    padded_rows = jnp.concatenate([embedded[sort_order], jnp.zeros((SLOTS, K), embedded.dtype)], 0)
    padded_band = jnp.concatenate([kernel_width[sort_order], jnp.zeros((SLOTS,), kernel_width.dtype)], 0)

    def one_cluster(cluster_index):
        block_start = starts[cluster_index].astype(jnp.int32)
        rows_block = lax.dynamic_slice_in_dim(padded_rows, block_start, SLOTS, 0)
        band_block = lax.dynamic_slice_in_dim(padded_band, block_start, SLOTS, 0)
        present = jnp.arange(SLOTS, dtype=jnp.int32) < counts[cluster_index]
        band_block = jnp.where(present, band_block, jnp.zeros_like(band_block))
        return diffuse(rows_block, band_block)

    blocks = lax.map(one_cluster, jnp.arange(CLUSTERS, dtype=jnp.int32))
    position = jnp.argsort(sort_order).astype(jnp.int32)
    safe_ids = jnp.minimum(keyed_ids, CLUSTERS - 1).astype(jnp.int32)
    flat_index = jnp.clip(safe_ids * SLOTS + position - starts[safe_ids], 0, CLUSTERS * SLOTS - 1).astype(jnp.int32)
    gathered = blocks.reshape(CLUSTERS * SLOTS, K)[flat_index]
    return jnp.where(is_live[:, None], gathered, embedded.astype(jnp.float32))
```

```python
import functools

import jax
import jax.numpy as jnp
from jax import lax
from jax.experimental import pallas as pl
from jax.experimental.pallas import tpu as pltpu
from jax.sharding import PartitionSpec as P

AXES = ("cells", "genes")
LANES = 128
LOG2E = 1.4426950408889634
FAR = 1e30
NT = (((1,), (1,)), ((), ()))
VMEM = pl.BlockSpec(memory_space=pltpu.VMEM)
SMEM = pl.BlockSpec(memory_space=pltpu.SMEM)
ANY = pl.BlockSpec(memory_space=pl.ANY)


def project_kernel(chunks, part_ref, x_ref, loading_ref, out_ref, buf, sems):
    rows = out_ref.shape[0] // chunks
    base = part_ref[0] * out_ref.shape[0]
    copies = []
    for k in range(chunks):
        start = pl.multiple_of(base + k * rows, rows)
        copies.append(
            pltpu.make_async_copy(x_ref.at[pl.ds(start, rows), :], buf.at[k], sems.at[k])
        )
        copies[-1].start()
    for k in range(chunks):
        copies[k].wait()
        out_ref[pl.ds(k * rows, rows), :] = jnp.dot(
            buf[k], loading_ref[...], preferred_element_type=jnp.float32
        )


def project(part, expression, loading, rows):
    genes, width = loading.shape
    chunks = 8
    return pl.pallas_call(
        functools.partial(project_kernel, chunks),
        out_shape=jax.ShapeDtypeStruct((rows, width), jnp.float32),
        in_specs=[SMEM, ANY, VMEM],
        out_specs=VMEM,
        scratch_shapes=[
            pltpu.VMEM((chunks, rows // chunks, genes), expression.dtype),
            pltpu.SemaphoreType.DMA((chunks,)),
        ],
        cost_estimate=pl.CostEstimate(
            flops=2 * rows * genes * width,
            bytes_accessed=2 * genes * (rows + width),
            transcendentals=0,
        ),
        name="project",
    )(part, expression, loading)


def iota(shape, axis):
    return lax.broadcasted_iota(jnp.int32, shape, axis)


def slots_of(cluster_row, quality_row, n_dest):
    cells = cluster_row.shape[1]
    member = (iota((n_dest, cells), 0) == cluster_row) & (quality_row == 1)
    ones = jnp.where(member, 1.0, 0.0)
    earlier = jnp.where(iota((cells, cells), 0) < iota((cells, cells), 1), 1.0, 0.0)
    before = jnp.dot(
        ones.astype(jnp.bfloat16), earlier.astype(jnp.bfloat16), preferred_element_type=jnp.float32
    )
    rank = jnp.sum(before * ones, axis=0, keepdims=True).astype(jnp.int32)
    return ones, rank


def pack_kernel(cap, cluster_ref, quality_ref, width_ref, *refs):
    *parts, packed_ref, embedded_ref, slot_ref = refs
    n_dest, stride, _ = packed_ref.shape
    cells = embedded_ref.shape[0]
    cluster_row = cluster_ref[...]
    quality_row = quality_ref[...]
    ones, rank = slots_of(cluster_row, quality_row, n_dest)
    live = quality_row == 1
    slot = jnp.where(live, cluster_row * cap + rank, -1)
    slot_ref[...] = jnp.broadcast_to(slot, slot_ref.shape)
    total = parts[0][...]
    for part in parts[1:]:
        total = total + part[...]
    embedded = total.astype(jnp.bfloat16)
    embedded_ref[...] = embedded
    place = jnp.where(live, cluster_row * stride + rank, -1)
    onehot = jnp.where(iota((n_dest * stride, cells), 0) == place, 1.0, 0.0).astype(jnp.bfloat16)
    rows = jnp.dot(onehot, embedded, preferred_element_type=jnp.float32)
    same_rank = jnp.where(lax.rem(iota((LANES, cells), 0), cap) == rank, 1.0, 0.0)
    owned = (ones * width_ref[...].astype(jnp.float32)).astype(jnp.bfloat16)
    widths = lax.dot_general(
        owned, same_rank.astype(jnp.bfloat16), NT, preferred_element_type=jnp.float32
    )
    rows = rows.reshape(packed_ref.shape)
    rows = jnp.where(iota(rows.shape, 1) >= cap, widths[:, None, :], rows)
    packed_ref[...] = rows.astype(jnp.bfloat16)


def diffuse_kernel(row_block, rows_ref, width_ref, out_ref, left, right, gain, affinity, step):
    slots = rows_ref.shape[0]
    sources = width_ref.shape[0]
    groups = slots // LANES
    per = sources // groups
    widths = width_ref[...].astype(jnp.float32).reshape(groups, per, LANES)
    mine = lax.div(iota(widths.shape, 2), LANES // per) == iota(widths.shape, 1)
    widths = jnp.sum(jnp.where(mine, widths, 0.0), axis=1)
    present = widths > 0
    inverse = jnp.where(present, 1.0 / jnp.where(present, widths, 1.0), 1.0)
    absent_col = jnp.transpose(jnp.where(present, 0.0, 1.0))
    gain_col = jnp.transpose(inverse * -LOG2E)
    lane = iota((LANES, LANES), 1)
    for g in range(groups):
        block = pl.ds(g * LANES, LANES)
        rows = rows_ref[block, :]
        wide = rows.astype(jnp.float32)
        norm = jnp.sum(wide * wide, axis=1, keepdims=True) + absent_col[:, g : g + 1] * FAR
        high = norm.astype(jnp.bfloat16).astype(jnp.float32)
        middle = (norm - high).astype(jnp.bfloat16).astype(jnp.float32)
        low = norm - high - middle
        one = jnp.ones_like(norm)
        split = jnp.where(lane == 0, high, jnp.where(lane == 1, middle, low))
        left[block, :LANES] = rows
        right[block, :LANES] = (wide * -2.0).astype(jnp.bfloat16)
        left[block, LANES:] = jnp.where(
            lane < 3, split, jnp.where(lane < 6, one, 0.0)
        ).astype(jnp.bfloat16)
        split = jnp.where(lane == 3, high, jnp.where(lane == 4, middle, low))
        right[block, LANES:] = jnp.where(
            lane < 3, one, jnp.where(lane < 6, split, 0.0)
        ).astype(jnp.bfloat16)
        gain[block, :] = jnp.broadcast_to(gain_col[:, g : g + 1], (LANES, LANES))
        step[block, :LANES] = rows
        step[block, LANES:] = jnp.ones((LANES, LANES), jnp.bfloat16)
    inverse_row = jnp.concatenate([inverse[g : g + 1, :] for g in range(groups)], axis=1)
    blocks = [pl.ds(b * row_block, row_block) for b in range(slots // row_block)]
    ones_steps, totals = [], []
    for block in blocks:
        distance = lax.dot_general(
            left[block, :], right[...], NT, preferred_element_type=jnp.float32
        )
        power = distance * gain[block, :1] * inverse_row
        weights = jnp.exp2(power).astype(jnp.bfloat16)
        affinity[block, :] = weights
        both = jnp.dot(weights, step[...], preferred_element_type=jnp.float32)
        total = both[:, LANES:]
        total = jnp.where(total > 0, total, 1.0)
        scale = 1.0 / total
        ones_steps.append(0.5 * (rows_ref[block, :].astype(jnp.float32) + both[:, :LANES] * scale))
        totals.append(scale)
    for block, one_step in zip(blocks, ones_steps):
        step[block, :LANES] = one_step.astype(jnp.bfloat16)
    for block, one_step, scale in zip(blocks, ones_steps, totals):
        again = jnp.dot(affinity[block, :], step[:, :LANES], preferred_element_type=jnp.float32)
        out_ref[block, :] = (0.5 * (one_step + again * scale)).astype(out_ref.dtype)


def diffuse(rows, widths):
    slots, width = rows.shape
    return pl.pallas_call(
        functools.partial(diffuse_kernel, 256),
        out_shape=jax.ShapeDtypeStruct((slots, width), jnp.bfloat16),
        in_specs=[VMEM] * 2,
        out_specs=VMEM,
        scratch_shapes=[
            pltpu.VMEM((slots, 2 * width), jnp.bfloat16),
            pltpu.VMEM((slots, 2 * width), jnp.bfloat16),
            pltpu.VMEM((slots, LANES), jnp.float32),
            pltpu.VMEM((slots, slots), jnp.bfloat16),
            pltpu.VMEM((slots, 2 * width), jnp.bfloat16),
        ],
        name="diffuse",
    )(rows, widths)


def pick_kernel(slot_ref, returned_ref, embedded_ref, out_ref):
    slot = jnp.transpose(slot_ref[...])[:, :1]
    shape = (slot.shape[0], returned_ref.shape[0])
    onehot = jnp.where(iota(shape, 1) == slot, 1.0, 0.0).astype(jnp.bfloat16)
    picked = jnp.dot(onehot, returned_ref[...], preferred_element_type=jnp.float32)
    out_ref[...] = jnp.where(slot >= 0, picked, embedded_ref[...].astype(jnp.float32))


def body(expression, loading, kernel_width, cluster, quality):
    gene_count = lax.axis_size("genes")
    devices = gene_count * lax.axis_size("cells")
    local = kernel_width.shape[0]
    cap = max(1, 2 * local // devices)
    stride = 8 * (cap // 8 + 1)
    width = loading.shape[1]
    me = lax.axis_index("genes")
    parts = []
    for shift in range(1, gene_count):
        part = lax.rem(me + shift, gene_count).reshape(1)
        ring = [(i, (i + shift) % gene_count) for i in range(gene_count)]
        parts.append(lax.ppermute(project(part, expression, loading, local), "genes", ring))
    parts.append(project(me.reshape(1), expression, loading, local))
    packed, embedded, slot = pl.pallas_call(
        functools.partial(pack_kernel, cap),
        out_shape=[
            jax.ShapeDtypeStruct((devices, stride, width), jnp.bfloat16),
            jax.ShapeDtypeStruct((local, width), jnp.bfloat16),
            jax.ShapeDtypeStruct((8, local), jnp.int32),
        ],
        in_specs=[VMEM] * (3 + len(parts)),
        out_specs=[VMEM] * 3,
        name="pack",
    )(
        cluster.reshape(1, local),
        quality.reshape(1, local),
        kernel_width.reshape(1, local),
        *parts,
    )
    arrived = lax.all_to_all(packed, AXES, split_axis=0, concat_axis=0, tiled=True)
    rows = arrived[:, :cap, :].reshape(devices * cap, width)
    smoothed = diffuse(rows, arrived[:, cap, :])
    returned = lax.all_to_all(
        smoothed.reshape(devices, cap, width), AXES, split_axis=0, concat_axis=0, tiled=True
    )
    return pl.pallas_call(
        pick_kernel,
        out_shape=jax.ShapeDtypeStruct((local, width), jnp.float32),
        in_specs=[VMEM] * 3,
        out_specs=VMEM,
        name="pick",
    )(slot, returned.reshape(devices * cap, width), embedded)


def solution(mesh):
    return jax.shard_map(
        body,
        mesh=mesh,
        in_specs=(
            P("cells", "genes"),
            P("genes", None),
            P(AXES),
            P(AXES, None),
            P(AXES),
        ),
        out_specs=P(AXES, None),
        check_vma=False,
    )
```

```python
import functools

import jax
import jax.numpy as jnp
from jax import lax
from jax.experimental import pallas as pl
from jax.experimental.pallas import tpu as pltpu
from jax.sharding import PartitionSpec as P

AXES = ("cells", "genes")
LANES = 128
LOG2E = 1.4426950408889634
FAR = 1e30
NT = (((1,), (1,)), ((), ()))
VMEM = pl.BlockSpec(memory_space=pltpu.VMEM)
HBM = pl.BlockSpec(memory_space=pltpu.HBM)
CHUNKS = 1


def grant(mebibytes):
    return pltpu.CompilerParams(vmem_limit_bytes=mebibytes << 20)


def iota(shape, axis):
    return lax.broadcasted_iota(jnp.int32, shape, axis)


def ranks(cluster_row, live, clusters):
    cells = cluster_row.shape[1]
    member = jnp.where((iota((clusters, cells), 0) == cluster_row) & live, 1.0, 0.0)
    earlier = jnp.where(iota((cells, cells), 0) < iota((cells, cells), 1), 1.0, 0.0)
    before = jnp.dot(
        member.astype(jnp.bfloat16),
        earlier.astype(jnp.bfloat16),
        preferred_element_type=jnp.float32,
    )
    return jnp.sum(before * member, axis=0, keepdims=True).astype(jnp.int32)


def project_kernel(stride, x_ref, loading_ref, cluster_ref, quality_ref, *refs):
    own_ref, weights_ref, place_ref, rank_ref, *out_refs, x_buf, labels, sems = refs
    parts = len(out_refs) + 1
    rows = own_ref.shape[0]
    depth = rows // CHUNKS
    me = lax.axis_index("genes")
    small = [
        pltpu.make_async_copy(cluster_ref, labels.at[0], sems.at[0, CHUNKS]),
        pltpu.make_async_copy(quality_ref, labels.at[1], sems.at[1, CHUNKS]),
    ]
    weights = pltpu.make_async_copy(loading_ref, weights_ref, sems.at[parts, CHUNKS])
    for copy in [*small, weights]:
        copy.start()
    copies = []
    for p in range(parts):
        buffer = own_ref if p == parts - 1 else x_buf.at[p]
        first = lax.rem(me + p + 1, parts) * rows
        copies.append([])
        for c in range(CHUNKS):
            source = x_ref.at[pl.ds(pl.multiple_of(first + c * depth, depth), depth), :]
            target = buffer.at[pl.ds(c * depth, depth), :]
            copies[p].append(pltpu.make_async_copy(source, target, sems.at[p, c]))
            copies[p][c].start()
    for copy in small:
        copy.wait()
    cluster_row = labels[0]
    live = labels[1] == 1
    rank = ranks(cluster_row, live, place_ref.shape[0] // stride)
    rank_ref[...] = jnp.broadcast_to(rank, rank_ref.shape)
    place = jnp.where(live, cluster_row * stride + rank, -1)
    place_ref[...] = jnp.where(iota(place_ref.shape, 0) == place, 1.0, 0.0).astype(jnp.bfloat16)
    weights.wait()
    for p in range(parts):
        for copy in copies[p]:
            copy.wait()
        if p < parts - 1:
            out_refs[p][...] = jnp.dot(
                x_buf[p], weights_ref[...], preferred_element_type=jnp.float32
            )


def project(expression, loading, cluster, quality, parts, devices, stride):
    cells, genes = expression.shape
    width = loading.shape[1]
    rows = cells // parts
    others = parts - 1
    operands = (expression, loading, cluster.reshape(1, rows), quality.reshape(1, rows))
    return pl.pallas_call(
        functools.partial(project_kernel, stride),
        out_shape=[
            jax.ShapeDtypeStruct((rows, genes), expression.dtype),
            jax.ShapeDtypeStruct((genes, width), loading.dtype),
            jax.ShapeDtypeStruct((devices * stride, rows), jnp.bfloat16),
            jax.ShapeDtypeStruct((8, rows), jnp.int32),
        ]
        + [jax.ShapeDtypeStruct((rows, width), jnp.float32)] * others,
        in_specs=[HBM] * 4,
        out_specs=[VMEM] * (4 + others),
        scratch_shapes=[
            pltpu.VMEM((max(others, 1), rows, genes), expression.dtype),
            pltpu.VMEM((2, 1, rows), jnp.int32),
            pltpu.SemaphoreType.DMA((parts + 1, CHUNKS + 1)),
        ],
        compiler_params=grant(24),
        name="project",
    )(*[pltpu.with_memory_space_constraint(operand, pltpu.HBM) for operand in operands])


def project_own_kernel(cap, x_ref, weights_ref, cluster_ref, quality_ref, rank_ref, width_ref, *refs):
    out_ref, spare_ref, pick_ref = refs
    out_ref[...] = jnp.dot(x_ref[...], weights_ref[...], preferred_element_type=jnp.float32)
    cells = x_ref.shape[0]
    live = quality_ref[...] == 1
    widths = jnp.where(live, width_ref[...].astype(jnp.float32), 0.0)
    rank = rank_ref[:1, :]
    slot = jnp.where(live, cluster_ref[...] * cap + rank, -1)
    slot = jnp.transpose(jnp.broadcast_to(slot, (8, cells)))[:, :1]
    pick_ref[...] = jnp.where(iota(pick_ref.shape, 1) == slot, 1.0, 0.0).astype(jnp.bfloat16)
    member = iota((spare_ref.shape[0], cells), 0) == cluster_ref[...]
    owned = jnp.where(member, widths, 0.0).astype(jnp.bfloat16)
    same_rank = jnp.where(lax.rem(iota((LANES, cells), 0), cap) == rank, 1.0, 0.0)
    spare_ref[...] = lax.dot_general(
        owned, same_rank.astype(jnp.bfloat16), NT, preferred_element_type=jnp.float32
    )


def project_own(own, weights, cluster, quality, rank, kernel_width, devices, cap):
    rows, genes = own.shape
    width = weights.shape[1]
    return pl.pallas_call(
        functools.partial(project_own_kernel, cap),
        out_shape=[
            jax.ShapeDtypeStruct((rows, width), jnp.float32),
            jax.ShapeDtypeStruct((devices, LANES), jnp.float32),
            jax.ShapeDtypeStruct((rows, devices * cap), jnp.bfloat16),
        ],
        in_specs=[VMEM] * 6,
        out_specs=[VMEM] * 3,
        cost_estimate=pl.CostEstimate(
            flops=2 * rows * genes * width,
            bytes_accessed=2 * genes * (rows + width),
            transcendentals=0,
        ),
        compiler_params=grant(10),
        name="project_own",
    )(
        own,
        weights,
        cluster.reshape(1, rows),
        quality.reshape(1, rows),
        rank,
        kernel_width.reshape(1, rows),
    )


def pack_kernel(cap, place_ref, spare_ref, *refs):
    *parts, packed_ref, embedded_ref = refs
    total = parts[0][...]
    for part in parts[1:]:
        total = total + part[...]
    embedded = total.astype(jnp.bfloat16)
    embedded_ref[...] = embedded
    rows = jnp.dot(place_ref[...], embedded, preferred_element_type=jnp.float32)
    rows = rows.reshape(packed_ref.shape)
    rows = jnp.where(iota(rows.shape, 1) >= cap, spare_ref[...][:, None, :], rows)
    packed_ref[...] = rows.astype(jnp.bfloat16)


def pack(parts, place, spare, cap, stride):
    cells, width = parts[0].shape
    return pl.pallas_call(
        functools.partial(pack_kernel, cap),
        out_shape=[
            jax.ShapeDtypeStruct((spare.shape[0], stride, width), jnp.bfloat16),
            jax.ShapeDtypeStruct((cells, width), jnp.bfloat16),
        ],
        in_specs=[VMEM] * (2 + len(parts)),
        out_specs=[VMEM] * 2,
        compiler_params=grant(10),
        name="pack",
    )(place, spare, *parts)


def diffuse_kernel(row_block, cap, arrived_ref, out_ref, left, right, gain, affinity, step):
    sources = arrived_ref.shape[0]
    slots = out_ref.shape[0]
    groups = slots // LANES
    per = LANES // cap
    widths = arrived_ref[:, cap, :].astype(jnp.float32).reshape(groups, per, LANES)
    mine = lax.div(iota(widths.shape, 2), LANES // per) == iota(widths.shape, 1)
    widths = jnp.sum(jnp.where(mine, widths, 0.0), axis=1)
    present = widths > 0
    inverse = jnp.where(present, 1.0 / jnp.where(present, widths, 1.0), 1.0)
    absent_col = jnp.transpose(jnp.where(present, 0.0, 1.0))
    gain_col = jnp.transpose(inverse * -LOG2E)
    lane = iota((LANES, LANES), 1)
    for g in range(groups):
        block = pl.ds(g * LANES, LANES)
        rows = jnp.concatenate(
            [arrived_ref[s, :cap, :] for s in range(g * per, (g + 1) * per)], axis=0
        )
        wide = rows.astype(jnp.float32)
        norm = jnp.sum(wide * wide, axis=1, keepdims=True) + absent_col[:, g : g + 1] * FAR
        high = norm.astype(jnp.bfloat16).astype(jnp.float32)
        middle = (norm - high).astype(jnp.bfloat16).astype(jnp.float32)
        low = norm - high - middle
        one = jnp.ones_like(norm)
        split = jnp.where(lane == 0, high, jnp.where(lane == 1, middle, low))
        left[block, :LANES] = rows
        right[block, :LANES] = (wide * -2.0).astype(jnp.bfloat16)
        left[block, LANES:] = jnp.where(
            lane < 3, split, jnp.where(lane < 6, one, 0.0)
        ).astype(jnp.bfloat16)
        split = jnp.where(lane == 3, high, jnp.where(lane == 4, middle, low))
        right[block, LANES:] = jnp.where(
            lane < 3, one, jnp.where(lane < 6, split, 0.0)
        ).astype(jnp.bfloat16)
        gain[block, :] = jnp.broadcast_to(gain_col[:, g : g + 1], (LANES, LANES))
        step[block, :LANES] = rows
        step[block, LANES:] = jnp.ones((LANES, LANES), jnp.bfloat16)
    inverse_row = jnp.concatenate([inverse[g : g + 1, :] for g in range(groups)], axis=1)
    blocks = [pl.ds(b * row_block, row_block) for b in range(slots // row_block)]
    ones_steps, totals = [], []
    for block in blocks:
        distance = lax.dot_general(
            left[block, :], right[...], NT, preferred_element_type=jnp.float32
        )
        power = distance * gain[block, :1] * inverse_row
        weights = jnp.exp2(power).astype(jnp.bfloat16)
        affinity[block, :] = weights
        both = jnp.dot(weights, step[...], preferred_element_type=jnp.float32)
        total = both[:, LANES:]
        total = jnp.where(total > 0, total, 1.0)
        scale = 1.0 / total
        ones_steps.append(0.5 * (left[block, :LANES].astype(jnp.float32) + both[:, :LANES] * scale))
        totals.append(scale)
    for block, one_step in zip(blocks, ones_steps):
        step[block, :LANES] = one_step.astype(jnp.bfloat16)
    for block, one_step, scale in zip(blocks, ones_steps, totals):
        again = jnp.dot(affinity[block, :], step[:, :LANES], preferred_element_type=jnp.float32)
        out_ref[block, :] = (0.5 * (one_step + again * scale)).astype(out_ref.dtype)


def diffuse(arrived, cap):
    sources, _, width = arrived.shape
    slots = sources * cap
    return pl.pallas_call(
        functools.partial(diffuse_kernel, 256, cap),
        out_shape=jax.ShapeDtypeStruct((slots, width), jnp.bfloat16),
        in_specs=[VMEM],
        out_specs=VMEM,
        scratch_shapes=[
            pltpu.VMEM((slots, 2 * width), jnp.bfloat16),
            pltpu.VMEM((slots, 2 * width), jnp.bfloat16),
            pltpu.VMEM((slots, LANES), jnp.float32),
            pltpu.VMEM((slots, slots), jnp.bfloat16),
            pltpu.VMEM((slots, 2 * width), jnp.bfloat16),
        ],
        compiler_params=grant(16),
        name="diffuse",
    )(arrived)


def pick_kernel(quality_ref, pick_ref, returned_ref, embedded_ref, out_ref):
    picked = jnp.dot(pick_ref[...], returned_ref[...], preferred_element_type=jnp.float32)
    live = jnp.transpose(jnp.broadcast_to(quality_ref[...], (8, out_ref.shape[0])))[:, :1] == 1
    out_ref[...] = jnp.where(live, picked, embedded_ref[...].astype(jnp.float32))


def pick(quality, pick_onehot, returned, embedded):
    cells, width = embedded.shape
    return pl.pallas_call(
        pick_kernel,
        out_shape=jax.ShapeDtypeStruct((cells, width), jnp.float32),
        in_specs=[VMEM] * 4,
        out_specs=VMEM,
        compiler_params=grant(8),
        name="pick",
    )(quality.reshape(1, cells), pick_onehot, returned, embedded)


def body(expression, loading, kernel_width, cluster, quality):
    gene_count = lax.axis_size("genes")
    devices = gene_count * lax.axis_size("cells")
    cap = max(1, 2 * kernel_width.shape[0] // devices)
    stride = 8 * (cap // 8 + 1)
    width = loading.shape[1]
    own, weights, place, rank, *partials = project(
        expression, loading, cluster, quality, gene_count, devices, stride
    )
    parts = []
    for shift, partial in enumerate(partials, 1):
        ring = [(i, (i + shift) % gene_count) for i in range(gene_count)]
        parts.append(lax.ppermute(partial, "genes", ring))
    own_part, spare, pick_onehot = project_own(
        own, weights, cluster, quality, rank, kernel_width, devices, cap
    )
    parts.append(own_part)
    packed, embedded = pack(parts, place, spare, cap, stride)
    arrived = lax.all_to_all(packed, AXES, split_axis=0, concat_axis=0, tiled=True)
    smoothed = diffuse(arrived, cap)
    returned = lax.all_to_all(
        smoothed.reshape(devices, cap, width), AXES, split_axis=0, concat_axis=0, tiled=True
    )
    return pick(quality, pick_onehot, returned.reshape(devices * cap, width), embedded)


def solution(mesh):
    return jax.shard_map(
        body,
        mesh=mesh,
        in_specs=(
            P("cells", "genes"),
            P("genes", None),
            P(AXES),
            P(AXES, None),
            P(AXES),
        ),
        out_specs=P(AXES, None),
        check_vma=False,
    )
```

```python
import functools

import jax
import jax.numpy as jnp
from jax import lax
from jax.experimental import pallas as pl
from jax.experimental.pallas import tpu as pltpu
from jax.sharding import PartitionSpec as P

AXES = ("cells", "genes")
LANES = 128
LOG2E = 1.4426950408889634
FAR = 1e30
NT = (((1,), (1,)), ((), ()))
VMEM = pl.BlockSpec(memory_space=pltpu.VMEM)
HBM = pl.BlockSpec(memory_space=pltpu.HBM)
CHUNKS = 1
ROW_BLOCK = 512
PICK_CHUNKS = 2
SLAB = 2


def grant(mebibytes):
    return pltpu.CompilerParams(vmem_limit_bytes=mebibytes << 20)


def iota(shape, axis):
    return lax.broadcasted_iota(jnp.int32, shape, axis)


def ranks(cluster_row, live, clusters):
    cells = cluster_row.shape[1]
    member = jnp.where((iota((clusters, cells), 0) == cluster_row) & live, 1.0, 0.0)
    earlier = jnp.where(iota((cells, cells), 0) < iota((cells, cells), 1), 1.0, 0.0)
    before = jnp.dot(
        member.astype(jnp.bfloat16),
        earlier.astype(jnp.bfloat16),
        preferred_element_type=jnp.float32,
    )
    return jnp.sum(before * member, axis=0, keepdims=True).astype(jnp.int32)


def project_kernel(cap, x_ref, loading_ref, cluster_ref, quality_ref, *refs):
    own_ref, weights_ref, place_ref, rank_ref, *out_refs, x_buf, labels, sems = refs
    parts = len(out_refs) + 1
    rows = own_ref.shape[0]
    depth = rows // CHUNKS
    me = lax.axis_index("genes")
    small = [
        pltpu.make_async_copy(cluster_ref, labels.at[0], sems.at[0, CHUNKS]),
        pltpu.make_async_copy(quality_ref, labels.at[1], sems.at[1, CHUNKS]),
    ]
    weights = pltpu.make_async_copy(loading_ref, weights_ref, sems.at[parts, CHUNKS])
    for copy in [*small, weights]:
        copy.start()
    copies = []
    for p in range(parts):
        buffer = own_ref if p == parts - 1 else x_buf.at[p]
        first = lax.rem(me + p + 1, parts) * rows
        copies.append([])
        for c in range(CHUNKS):
            source = x_ref.at[pl.ds(pl.multiple_of(first + c * depth, depth), depth), :]
            target = buffer.at[pl.ds(c * depth, depth), :]
            copies[p].append(pltpu.make_async_copy(source, target, sems.at[p, c]))
            copies[p][c].start()
    for copy in small:
        copy.wait()
    cluster_row = labels[0]
    live = labels[1] == 1
    rank = ranks(cluster_row, live, place_ref.shape[0] // cap)
    rank_ref[...] = jnp.broadcast_to(rank, rank_ref.shape)
    place = jnp.where(live, cluster_row * cap + rank, -1)
    place_ref[...] = jnp.where(iota(place_ref.shape, 0) == place, 1.0, 0.0).astype(jnp.bfloat16)
    weights.wait()
    for p in range(parts):
        for copy in copies[p]:
            copy.wait()
        if p < parts - 1:
            out_refs[p][...] = jnp.dot(
                x_buf[p], weights_ref[...], preferred_element_type=jnp.float32
            )


def project(expression, loading, cluster, quality, parts, devices, cap):
    cells, genes = expression.shape
    width = loading.shape[1]
    rows = cells // parts
    others = parts - 1
    operands = (expression, loading, cluster.reshape(1, rows), quality.reshape(1, rows))
    return pl.pallas_call(
        functools.partial(project_kernel, cap),
        out_shape=[
            jax.ShapeDtypeStruct((rows, genes), expression.dtype),
            jax.ShapeDtypeStruct((genes, width), loading.dtype),
            jax.ShapeDtypeStruct((devices * cap, rows), jnp.bfloat16),
            jax.ShapeDtypeStruct((8, rows), jnp.int32),
        ]
        + [jax.ShapeDtypeStruct((rows, width), jnp.float32)] * others,
        in_specs=[HBM] * 4,
        out_specs=[VMEM] * (4 + others),
        scratch_shapes=[
            pltpu.VMEM((max(others, 1), rows, genes), expression.dtype),
            pltpu.VMEM((2, 1, rows), jnp.int32),
            pltpu.SemaphoreType.DMA((parts + 1, CHUNKS + 1)),
        ],
        compiler_params=grant(24),
        name="project",
    )(*[pltpu.with_memory_space_constraint(operand, pltpu.HBM) for operand in operands])


def project_own_kernel(cap, x_ref, weights_ref, cluster_ref, quality_ref, rank_ref, width_ref, *refs):
    out_ref, spare_ref, pick_ref = refs
    out_ref[...] = jnp.dot(x_ref[...], weights_ref[...], preferred_element_type=jnp.float32)
    cells = x_ref.shape[0]
    live = quality_ref[...] == 1
    widths = jnp.where(live, width_ref[...].astype(jnp.float32), 0.0)
    rank = rank_ref[:1, :]
    slot = jnp.where(live, cluster_ref[...] * cap + rank, -1)
    slot = jnp.transpose(jnp.broadcast_to(slot, (8, cells)))[:, :1]
    pick_ref[...] = jnp.where(iota(pick_ref.shape, 1) == slot, 1.0, 0.0).astype(jnp.bfloat16)
    member = iota((spare_ref.shape[0], cells), 0) == cluster_ref[...]
    owned = jnp.where(member, widths, 0.0).astype(jnp.bfloat16)
    same_rank = jnp.where(lax.rem(iota((LANES, cells), 0), cap) == rank, 1.0, 0.0)
    spare_ref[...] = lax.dot_general(
        owned, same_rank.astype(jnp.bfloat16), NT, preferred_element_type=jnp.float32
    )


def project_own(own, weights, cluster, quality, rank, kernel_width, devices, cap):
    rows, genes = own.shape
    width = weights.shape[1]
    return pl.pallas_call(
        functools.partial(project_own_kernel, cap),
        out_shape=[
            jax.ShapeDtypeStruct((rows, width), jnp.float32),
            jax.ShapeDtypeStruct((devices, LANES), jnp.float32),
            jax.ShapeDtypeStruct((rows, devices * cap), jnp.bfloat16),
        ],
        in_specs=[VMEM] * 6,
        out_specs=[VMEM] * 3,
        cost_estimate=pl.CostEstimate(
            flops=2 * rows * genes * width,
            bytes_accessed=2 * genes * (rows + width),
            transcendentals=0,
        ),
        compiler_params=grant(10),
        name="project_own",
    )(
        own,
        weights,
        cluster.reshape(1, rows),
        quality.reshape(1, rows),
        rank,
        kernel_width.reshape(1, rows),
    )


def pack_kernel(place_ref, spare_ref, *refs):
    *parts, packed_ref, embedded_ref = refs
    total = parts[0][...]
    for part in parts[1:]:
        total = total + part[...]
    embedded = total.astype(jnp.bfloat16)
    embedded_ref[...] = embedded
    rows = jnp.dot(place_ref[...], embedded, preferred_element_type=jnp.float32)
    n_dest, slabs, slab, width = packed_ref.shape
    rows = rows.reshape(n_dest, slabs - 1, slab, width)
    packed_ref[:, : slabs - 1] = rows.astype(jnp.bfloat16)
    spare = jnp.broadcast_to(spare_ref[...][:, None, None, :], (n_dest, 1, slab, width))
    packed_ref[:, slabs - 1 :] = spare.astype(jnp.bfloat16)


def pack(parts, place, spare, cap):
    cells, width = parts[0].shape
    return pl.pallas_call(
        pack_kernel,
        out_shape=[
            jax.ShapeDtypeStruct((spare.shape[0], cap // SLAB + 1, SLAB, width), jnp.bfloat16),
            jax.ShapeDtypeStruct((cells, width), jnp.bfloat16),
        ],
        in_specs=[VMEM] * (2 + len(parts)),
        out_specs=[VMEM] * 2,
        compiler_params=grant(10),
        name="pack",
    )(place, spare, *parts)


def diffuse_kernel(row_block, cap, arrived_ref, out_ref, rows, affinity, step):
    slots, width = out_ref.shape
    slabs = arrived_ref.shape[1] - 1
    groups = slots // LANES
    per = LANES // cap
    shape = (groups, LANES)
    source = lax.div(iota(shape, 1), cap)
    diagonal = iota((LANES, LANES), 0) == iota((LANES, LANES), 1)
    widths = jnp.zeros(shape, jnp.float32)
    half_norms = jnp.zeros(shape, jnp.float32)
    rows[:, :width] = arrived_ref[:, :slabs].reshape(slots, width)
    for g in range(groups):
        block = pl.ds(g * LANES, LANES)
        line = jnp.zeros(shape, jnp.float32)
        for q in range(per):
            last = arrived_ref[g * per + q, slabs].astype(jnp.float32)[:1, :]
            line = jnp.where(source == q, last, line)
        embedded = rows[block, :width]
        rows[block, width:] = jnp.ones((LANES, LANES), jnp.bfloat16)
        own = lax.dot_general(embedded, embedded, NT, preferred_element_type=jnp.float32)
        norm = jnp.sum(jnp.where(diagonal, own, 0.0), axis=0, keepdims=True)
        here = iota(shape, 0) == g
        widths = jnp.where(here, line, widths)
        half_norms = jnp.where(here, 0.5 * norm, half_norms)
    present = widths > 0
    half_norms = jnp.where(present, half_norms, FAR)
    inverse = jnp.where(present, 1.0 / jnp.where(present, widths, 1.0), 1.0)
    norm_cols = jnp.transpose(half_norms)
    gain_cols = jnp.transpose(inverse * (2.0 * LOG2E))

    def across(lines):
        return jnp.concatenate([lines[g : g + 1, :] for g in range(groups)], axis=1)

    def down(cols, b):
        first, count = b * row_block // LANES, row_block // LANES
        return jnp.concatenate([cols[:, g : g + 1] for g in range(first, first + count)], axis=0)

    norm_row, inverse_row = across(half_norms), across(inverse)
    blocks = [pl.ds(b * row_block, row_block) for b in range(slots // row_block)]
    one_steps, scales = [], []
    for b, block in enumerate(blocks):
        products = lax.dot_general(
            rows[block, :width], rows[:, :width], NT, preferred_element_type=jnp.float32
        )
        power = (products - norm_row - down(norm_cols, b)) * (down(gain_cols, b) * inverse_row)
        weights = jnp.exp2(power).astype(jnp.bfloat16)
        affinity[block, :] = weights
        both = jnp.dot(weights, rows[...], preferred_element_type=jnp.float32)
        total = both[:, width:]
        scale = 1.0 / jnp.where(total > 0, total, 1.0)
        one_step = 0.5 * (rows[block, :width].astype(jnp.float32) + both[:, :width] * scale)
        step[block, :] = one_step.astype(jnp.bfloat16)
        one_steps.append(one_step)
        scales.append(scale)
    for block, one_step, scale in zip(blocks, one_steps, scales):
        again = jnp.dot(affinity[block, :], step[...], preferred_element_type=jnp.float32)
        out_ref[block, :] = (0.5 * (one_step + again * scale)).astype(out_ref.dtype)


def diffuse(arrived, cap):
    sources, _, _, width = arrived.shape
    slots = sources * cap
    return pl.pallas_call(
        functools.partial(diffuse_kernel, ROW_BLOCK, cap),
        out_shape=jax.ShapeDtypeStruct((slots, width), jnp.bfloat16),
        in_specs=[VMEM],
        out_specs=VMEM,
        scratch_shapes=[
            pltpu.VMEM((slots, width + LANES), jnp.bfloat16),
            pltpu.VMEM((slots, slots), jnp.bfloat16),
            pltpu.VMEM((slots, width), jnp.bfloat16),
        ],
        compiler_params=grant(16),
        name="diffuse",
    )(arrived)


def pick_kernel(quality_ref, pick_ref, returned_ref, embedded_ref, out_ref, buf, sems):
    cells = out_ref.shape[0]
    live = jnp.transpose(jnp.broadcast_to(quality_ref[...], (8, cells)))[:, :1] == 1
    depth = cells // PICK_CHUNKS
    copies = []
    for k in range(PICK_CHUNKS):
        block = pl.ds(k * depth, depth)
        picked = jnp.dot(pick_ref[block, :], returned_ref[...], preferred_element_type=jnp.float32)
        kept = embedded_ref[block, :].astype(jnp.float32)
        buf[block, :] = jnp.where(live[k * depth : (k + 1) * depth], picked, kept)
        copies.append(pltpu.make_async_copy(buf.at[block, :], out_ref.at[block, :], sems.at[k]))
        copies[k].start()
    for copy in copies:
        copy.wait()


def pick(quality, pick_onehot, returned, embedded):
    cells, width = embedded.shape
    return pl.pallas_call(
        pick_kernel,
        out_shape=jax.ShapeDtypeStruct((cells, width), jnp.float32),
        in_specs=[VMEM] * 4,
        out_specs=HBM,
        scratch_shapes=[
            pltpu.VMEM((cells, width), jnp.float32),
            pltpu.SemaphoreType.DMA((PICK_CHUNKS,)),
        ],
        compiler_params=grant(8),
        name="pick",
    )(quality.reshape(1, cells), pick_onehot, returned, embedded)


def body(expression, loading, kernel_width, cluster, quality):
    gene_count = lax.axis_size("genes")
    devices = gene_count * lax.axis_size("cells")
    cap = SLAB * pl.cdiv(max(1, 2 * kernel_width.shape[0] // devices), SLAB)
    width = loading.shape[1]
    own, weights, place, rank, *partials = project(
        expression, loading, cluster, quality, gene_count, devices, cap
    )
    parts = []
    for shift, partial in enumerate(partials, 1):
        ring = [(i, (i + shift) % gene_count) for i in range(gene_count)]
        parts.append(lax.ppermute(partial, "genes", ring))
    own_part, spare, pick_onehot = project_own(
        own, weights, cluster, quality, rank, kernel_width, devices, cap
    )
    parts.append(own_part)
    packed, embedded = pack(parts, place, spare, cap)
    arrived = lax.all_to_all(packed, AXES, split_axis=0, concat_axis=0, tiled=True)
    smoothed = diffuse(arrived, cap)
    returned = lax.all_to_all(
        smoothed.reshape(devices, cap, width), AXES, split_axis=0, concat_axis=0, tiled=True
    )
    return pick(quality, pick_onehot, returned.reshape(devices * cap, width), embedded)


def solution(mesh):
    return jax.shard_map(
        body,
        mesh=mesh,
        in_specs=(
            P("cells", "genes"),
            P("genes", None),
            P(AXES),
            P(AXES, None),
            P(AXES),
        ),
        out_specs=P(AXES, None),
        check_vma=False,
    )
```

```python
import functools

import jax
import jax.numpy as jnp
from jax import lax
from jax.experimental import pallas as pl
from jax.experimental.pallas import tpu as pltpu
from jax.sharding import PartitionSpec as P

AXES = ("cells", "genes")
LANES = 128
LOG2E = 1.4426950408889634
FAR = 1e30
NT = (((1,), (1,)), ((), ()))
VMEM = pl.BlockSpec(memory_space=pltpu.VMEM)
HBM = pl.BlockSpec(memory_space=pltpu.HBM)
CHUNKS = 1
ROW_BLOCK = 256
TALL_BLOCKS = 2
PICK_CHUNKS = 2
SLAB = 2


def grant(mebibytes):
    return pltpu.CompilerParams(vmem_limit_bytes=mebibytes << 20)


def iota(shape, axis):
    return lax.broadcasted_iota(jnp.int32, shape, axis)


def ranks(cluster_row, live, clusters):
    cells = cluster_row.shape[1]
    member = jnp.where((iota((clusters, cells), 0) == cluster_row) & live, 1.0, 0.0)
    earlier = jnp.where(iota((cells, cells), 0) < iota((cells, cells), 1), 1.0, 0.0)
    before = jnp.dot(
        member.astype(jnp.bfloat16),
        earlier.astype(jnp.bfloat16),
        preferred_element_type=jnp.float32,
    )
    return jnp.sum(before * member, axis=0, keepdims=True).astype(jnp.int32)


def project_kernel(cap, x_ref, loading_ref, cluster_ref, quality_ref, *refs):
    own_ref, weights_ref, place_ref, rank_ref, *out_refs, x_buf, labels, sems = refs
    parts = len(out_refs) + 1
    rows = own_ref.shape[0]
    depth = rows // CHUNKS
    me = lax.axis_index("genes")
    small = [
        pltpu.make_async_copy(cluster_ref, labels.at[0], sems.at[0, CHUNKS]),
        pltpu.make_async_copy(quality_ref, labels.at[1], sems.at[1, CHUNKS]),
    ]
    weights = pltpu.make_async_copy(loading_ref, weights_ref, sems.at[parts, CHUNKS])
    for copy in [*small, weights]:
        copy.start()
    copies = []
    for p in range(parts):
        buffer = own_ref if p == parts - 1 else x_buf.at[p]
        first = lax.rem(me + p + 1, parts) * rows
        copies.append([])
        for c in range(CHUNKS):
            source = x_ref.at[pl.ds(pl.multiple_of(first + c * depth, depth), depth), :]
            target = buffer.at[pl.ds(c * depth, depth), :]
            copies[p].append(pltpu.make_async_copy(source, target, sems.at[p, c]))
            copies[p][c].start()
    for copy in small:
        copy.wait()
    cluster_row = labels[0]
    live = labels[1] == 1
    half = place_ref.shape[0]
    rank = ranks(cluster_row, live, 2 * half // cap)
    rank_ref[...] = jnp.broadcast_to(rank, rank_ref.shape)
    place = jnp.where(live, lax.rem(cluster_row * cap + rank, half), -1)
    place_ref[...] = jnp.where(iota(place_ref.shape, 0) == place, 1.0, 0.0).astype(jnp.bfloat16)
    weights.wait()
    for p in range(parts):
        for copy in copies[p]:
            copy.wait()
        if p < parts - 1:
            out_refs[p][...] = jnp.dot(
                x_buf[p], weights_ref[...], preferred_element_type=jnp.float32
            )


def project(expression, loading, cluster, quality, parts, devices, cap):
    cells, genes = expression.shape
    width = loading.shape[1]
    rows = cells // parts
    others = parts - 1
    operands = (expression, loading, cluster.reshape(1, rows), quality.reshape(1, rows))
    return pl.pallas_call(
        functools.partial(project_kernel, cap),
        out_shape=[
            jax.ShapeDtypeStruct((rows, genes), expression.dtype),
            jax.ShapeDtypeStruct((genes, width), loading.dtype),
            jax.ShapeDtypeStruct((devices * cap // 2, rows), jnp.bfloat16),
            jax.ShapeDtypeStruct((8, rows), jnp.int32),
        ]
        + [jax.ShapeDtypeStruct((rows, width), jnp.float32)] * others,
        in_specs=[HBM] * 4,
        out_specs=[VMEM] * (4 + others),
        scratch_shapes=[
            pltpu.VMEM((max(others, 1), rows, genes), expression.dtype),
            pltpu.VMEM((2, 1, rows), jnp.int32),
            pltpu.SemaphoreType.DMA((parts + 1, CHUNKS + 1)),
        ],
        compiler_params=grant(24),
        name="project",
    )(*[pltpu.with_memory_space_constraint(operand, pltpu.HBM) for operand in operands])


def project_own_kernel(cap, x_ref, weights_ref, cluster_ref, quality_ref, rank_ref, width_ref, *refs):
    out_ref, spare_ref, pick_ref, side_ref = refs
    out_ref[...] = jnp.dot(x_ref[...], weights_ref[...], preferred_element_type=jnp.float32)
    cells = x_ref.shape[0]
    live = quality_ref[...] == 1
    widths = jnp.where(live, width_ref[...].astype(jnp.float32), 0.0)
    rank = rank_ref[:1, :]
    slot = jnp.where(live, cluster_ref[...] * cap + rank, -1)
    slot = jnp.transpose(jnp.broadcast_to(slot, (8, cells)))[:, :1]
    half = pick_ref.shape[1]
    side = jnp.where(slot < 0, -1, jnp.where(slot < half, 0, 1))
    side_ref[...] = jnp.broadcast_to(side, side_ref.shape)
    place = slot - jnp.maximum(side, 0) * half
    pick_ref[...] = jnp.where(iota(pick_ref.shape, 1) == place, 1.0, 0.0).astype(jnp.bfloat16)
    member = iota((spare_ref.shape[0], cells), 0) == cluster_ref[...]
    owned = jnp.where(member, widths, 0.0).astype(jnp.bfloat16)
    same_rank = jnp.where(lax.rem(iota((LANES, cells), 0), cap) == rank, 1.0, 0.0)
    spare_ref[...] = lax.dot_general(
        owned, same_rank.astype(jnp.bfloat16), NT, preferred_element_type=jnp.float32
    )


def project_own(own, weights, cluster, quality, rank, kernel_width, devices, cap):
    rows, genes = own.shape
    width = weights.shape[1]
    return pl.pallas_call(
        functools.partial(project_own_kernel, cap),
        out_shape=[
            jax.ShapeDtypeStruct((rows, width), jnp.float32),
            jax.ShapeDtypeStruct((devices, LANES), jnp.float32),
            jax.ShapeDtypeStruct((rows, devices * cap // 2), jnp.bfloat16),
            jax.ShapeDtypeStruct((rows, width), jnp.int32),
        ],
        in_specs=[VMEM] * 6,
        out_specs=[VMEM] * 4,
        cost_estimate=pl.CostEstimate(
            flops=2 * rows * genes * width,
            bytes_accessed=2 * genes * (rows + width),
            transcendentals=0,
        ),
        compiler_params=grant(10),
        name="project_own",
    )(
        own,
        weights,
        cluster.reshape(1, rows),
        quality.reshape(1, rows),
        rank,
        kernel_width.reshape(1, rows),
    )


def pack_kernel(place_ref, side_ref, spare_ref, *refs):
    *parts, packed_ref, embedded_ref = refs
    total = parts[0][...]
    for part in parts[1:]:
        total = total + part[...]
    embedded = total.astype(jnp.bfloat16)
    embedded_ref[...] = embedded
    side = side_ref[...]
    halves = [jnp.where(side == half, total, 0.0).astype(jnp.bfloat16) for half in range(2)]
    both = jnp.concatenate(halves, axis=1)
    rows = jnp.dot(place_ref[...], both, preferred_element_type=jnp.float32)
    n_dest, slabs, slab, width = packed_ref.shape
    for half in range(2):
        part = rows[:, half * width : (half + 1) * width].astype(jnp.bfloat16)
        part = part.reshape(n_dest // 2, slabs - 1, slab, width)
        packed_ref[half * n_dest // 2 : (half + 1) * n_dest // 2, : slabs - 1] = part
    spare = jnp.broadcast_to(spare_ref[...][:, None, None, :], (n_dest, 1, slab, width))
    packed_ref[:, slabs - 1 :] = spare.astype(jnp.bfloat16)


def pack(parts, place, side, spare, cap):
    cells, width = parts[0].shape
    return pl.pallas_call(
        pack_kernel,
        out_shape=[
            jax.ShapeDtypeStruct((spare.shape[0], cap // SLAB + 1, SLAB, width), jnp.bfloat16),
            jax.ShapeDtypeStruct((cells, width), jnp.bfloat16),
        ],
        in_specs=[VMEM] * (3 + len(parts)),
        out_specs=[VMEM] * 2,
        compiler_params=grant(10),
        name="pack",
    )(place, side, spare, *parts)


def diffuse_kernel(row_block, cap, arrived_ref, out_ref, rows, affinity, step):
    slots, width = out_ref.shape
    slabs = arrived_ref.shape[1] - 1
    groups = slots // LANES
    per = LANES // cap
    shape = (groups, LANES)
    source = lax.div(iota(shape, 1), cap)
    diagonal = iota((LANES, LANES), 0) == iota((LANES, LANES), 1)
    widths = jnp.zeros(shape, jnp.float32)
    half_norms = jnp.zeros(shape, jnp.float32)
    rows[:, :width] = arrived_ref[:, :slabs].reshape(slots, width)
    for g in range(groups):
        block = pl.ds(g * LANES, LANES)
        line = jnp.zeros(shape, jnp.float32)
        for q in range(per):
            last = arrived_ref[g * per + q, slabs].astype(jnp.float32)[:1, :]
            line = jnp.where(source == q, last, line)
        embedded = rows[block, :width]
        rows[block, width:] = jnp.ones((LANES, LANES), jnp.bfloat16)
        own = lax.dot_general(embedded, embedded, NT, preferred_element_type=jnp.float32)
        norm = jnp.sum(jnp.where(diagonal, own, 0.0), axis=0, keepdims=True)
        here = iota(shape, 0) == g
        widths = jnp.where(here, line, widths)
        half_norms = jnp.where(here, 0.5 * norm, half_norms)
    present = widths > 0
    half_norms = jnp.where(present, half_norms, FAR)
    inverse = jnp.where(present, 1.0 / jnp.where(present, widths, 1.0), 1.0)
    norm_cols = jnp.transpose(half_norms)
    gain_cols = jnp.transpose(inverse * (2.0 * LOG2E))

    def across(lines):
        return jnp.concatenate([lines[g : g + 1, :] for g in range(groups)], axis=1)

    def down(cols, b):
        first, count = b * row_block // LANES, row_block // LANES
        return jnp.concatenate([cols[:, g : g + 1] for g in range(first, first + count)], axis=0)

    norm_row, inverse_row = across(half_norms), across(inverse)
    blocks = [pl.ds(b * row_block, row_block) for b in range(slots // row_block)]
    one_steps, scales = [], []
    for b, block in enumerate(blocks):
        first = b * row_block
        beyond = pl.ds(first, slots - first)
        products = lax.dot_general(
            rows[block, :width], rows[beyond, :width], NT, preferred_element_type=jnp.float32
        )
        power = (products - norm_row[:, first:] - down(norm_cols, b)) * (
            down(gain_cols, b) * inverse_row[:, first:]
        )
        weights = jnp.exp2(power).astype(jnp.bfloat16)
        affinity[block, beyond] = weights
        for later in range(b + 1, len(blocks)):
            start = (later - b) * row_block
            affinity[blocks[later], block] = jnp.transpose(weights[:, start : start + row_block])
        weights = affinity[block, :]
        both = jnp.dot(weights, rows[...], preferred_element_type=jnp.float32)
        total = both[:, width:]
        scale = 1.0 / jnp.where(total > 0, total, 1.0)
        one_step = 0.5 * (rows[block, :width].astype(jnp.float32) + both[:, :width] * scale)
        step[block, :] = one_step.astype(jnp.bfloat16)
        one_steps.append(one_step)
        scales.append(scale)
    tall = slots // TALL_BLOCKS
    join = len(blocks) // TALL_BLOCKS
    for t in range(TALL_BLOCKS):
        block = pl.ds(t * tall, tall)
        again = jnp.dot(affinity[block, :], step[...], preferred_element_type=jnp.float32)
        for b in range(t * join, (t + 1) * join):
            start = b * row_block - t * tall
            more = again[start : start + row_block] * scales[b]
            out_ref[blocks[b], :] = (0.5 * (one_steps[b] + more)).astype(out_ref.dtype)


def diffuse(arrived, cap):
    sources, _, _, width = arrived.shape
    slots = sources * cap
    return pl.pallas_call(
        functools.partial(diffuse_kernel, ROW_BLOCK, cap),
        out_shape=jax.ShapeDtypeStruct((slots, width), jnp.bfloat16),
        in_specs=[VMEM],
        out_specs=VMEM,
        scratch_shapes=[
            pltpu.VMEM((slots, width + LANES), jnp.bfloat16),
            pltpu.VMEM((slots, slots), jnp.bfloat16),
            pltpu.VMEM((slots, width), jnp.bfloat16),
        ],
        compiler_params=grant(16),
        name="diffuse",
    )(arrived)


def pick_kernel(pick_ref, side_ref, returned_ref, embedded_ref, out_ref, buf, sems):
    cells, width = out_ref.shape
    half = pick_ref.shape[1]
    both = jnp.concatenate([returned_ref[:half, :], returned_ref[half:, :]], axis=1)
    depth = cells // PICK_CHUNKS
    copies = []
    for k in range(PICK_CHUNKS):
        block = pl.ds(k * depth, depth)
        picked = jnp.dot(pick_ref[block, :], both, preferred_element_type=jnp.float32)
        side = side_ref[block, :]
        kept = embedded_ref[block, :].astype(jnp.float32)
        second = jnp.where(side == 1, picked[:, width:], kept)
        buf[block, :] = jnp.where(side == 0, picked[:, :width], second)
        copies.append(pltpu.make_async_copy(buf.at[block, :], out_ref.at[block, :], sems.at[k]))
        copies[k].start()
    for copy in copies:
        copy.wait()


def pick(pick_onehot, side, returned, embedded):
    cells, width = embedded.shape
    return pl.pallas_call(
        pick_kernel,
        out_shape=jax.ShapeDtypeStruct((cells, width), jnp.float32),
        in_specs=[VMEM] * 4,
        out_specs=HBM,
        scratch_shapes=[
            pltpu.VMEM((cells, width), jnp.float32),
            pltpu.SemaphoreType.DMA((PICK_CHUNKS,)),
        ],
        compiler_params=grant(8),
        name="pick",
    )(pick_onehot, side, returned, embedded)


def body(expression, loading, kernel_width, cluster, quality):
    gene_count = lax.axis_size("genes")
    devices = gene_count * lax.axis_size("cells")
    cap = SLAB * pl.cdiv(max(1, 2 * kernel_width.shape[0] // devices), SLAB)
    width = loading.shape[1]
    own, weights, place, rank, *partials = project(
        expression, loading, cluster, quality, gene_count, devices, cap
    )
    parts = []
    for shift, partial in enumerate(partials, 1):
        ring = [(i, (i + shift) % gene_count) for i in range(gene_count)]
        parts.append(lax.ppermute(partial, "genes", ring))
    own_part, spare, pick_onehot, side = project_own(
        own, weights, cluster, quality, rank, kernel_width, devices, cap
    )
    parts.append(own_part)
    packed, embedded = pack(parts, place, side, spare, cap)
    arrived = lax.all_to_all(packed, AXES, split_axis=0, concat_axis=0, tiled=True)
    smoothed = diffuse(arrived, cap)
    returned = lax.all_to_all(
        smoothed.reshape(devices, cap, width), AXES, split_axis=0, concat_axis=0, tiled=True
    )
    return pick(pick_onehot, side, returned.reshape(devices * cap, width), embedded)


def solution(mesh):
    return jax.shard_map(
        body,
        mesh=mesh,
        in_specs=(
            P("cells", "genes"),
            P("genes", None),
            P(AXES),
            P(AXES, None),
            P(AXES),
        ),
        out_specs=P(AXES, None),
        check_vma=False,
    )
```

```python
import functools

import jax
import jax.numpy as jnp
from jax import lax
from jax.experimental import pallas as pl
from jax.experimental.pallas import tpu as pltpu
from jax.sharding import PartitionSpec as P

AXES = ("cells", "genes")
LANES = 128
LOG2E = 1.4426950408889634
FAR = 1e30
NT = (((1,), (1,)), ((), ()))
VMEM = pl.BlockSpec(memory_space=pltpu.VMEM)
HBM = pl.BlockSpec(memory_space=pltpu.HBM)
CHUNKS = 2
ROW_BLOCK = 256
TALL_BLOCKS = 2
PICK_CHUNKS = 2
SLAB = 2


def grant(mebibytes):
    return pltpu.CompilerParams(vmem_limit_bytes=mebibytes << 20)


def iota(shape, axis):
    return lax.broadcasted_iota(jnp.int32, shape, axis)


def ranks(cluster_row, live, clusters):
    cells = cluster_row.shape[1]
    member = jnp.where((iota((clusters, cells), 0) == cluster_row) & live, 1.0, 0.0)
    earlier = jnp.where(iota((cells, cells), 0) < iota((cells, cells), 1), 1.0, 0.0)
    before = jnp.dot(
        member.astype(jnp.bfloat16),
        earlier.astype(jnp.bfloat16),
        preferred_element_type=jnp.float32,
    )
    return jnp.sum(before * member, axis=0, keepdims=True).astype(jnp.int32)


def project_kernel(cap, x_ref, loading_ref, cluster_ref, quality_ref, *refs):
    own_ref, weights_ref, place_ref, rank_ref, *out_refs, x_buf, labels, sems = refs
    parts = len(out_refs) + 1
    rows = own_ref.shape[0]
    depth = rows // CHUNKS
    me = lax.axis_index("genes")
    small = [
        pltpu.make_async_copy(cluster_ref, labels.at[0], sems.at[0, CHUNKS]),
        pltpu.make_async_copy(quality_ref, labels.at[1], sems.at[1, CHUNKS]),
    ]
    weights = pltpu.make_async_copy(loading_ref, weights_ref, sems.at[parts, CHUNKS])
    for copy in [*small, weights]:
        copy.start()
    copies = []
    for p in range(parts):
        buffer = own_ref if p == parts - 1 else x_buf.at[pl.ds(p * rows, rows), :]
        first = lax.rem(me + p + 1, parts) * rows
        copies.append([])
        for c in range(CHUNKS):
            source = x_ref.at[pl.ds(pl.multiple_of(first + c * depth, depth), depth), :]
            target = buffer.at[pl.ds(c * depth, depth), :]
            copies[p].append(pltpu.make_async_copy(source, target, sems.at[p, c]))
            copies[p][c].start()
    for copy in small:
        copy.wait()
    cluster_row = labels[0]
    live = labels[1] == 1
    half = place_ref.shape[0]
    rank = ranks(cluster_row, live, 2 * half // cap)
    rank_ref[...] = jnp.broadcast_to(rank, rank_ref.shape)
    place = jnp.where(live, lax.rem(cluster_row * cap + rank, half), -1)
    place_ref[...] = jnp.where(iota(place_ref.shape, 0) == place, 1.0, 0.0).astype(jnp.bfloat16)
    weights.wait()
    for p in range(parts):
        for c, copy in enumerate(copies[p]):
            copy.wait()
            if p < parts - 1:
                out_refs[p][pl.ds(c * depth, depth), :] = jnp.dot(
                    x_buf[pl.ds(p * rows + c * depth, depth), :],
                    weights_ref[...],
                    preferred_element_type=jnp.float32,
                )


def project(expression, loading, cluster, quality, parts, devices, cap):
    cells, genes = expression.shape
    width = loading.shape[1]
    rows = cells // parts
    others = parts - 1
    operands = (expression, loading, cluster.reshape(1, rows), quality.reshape(1, rows))
    return pl.pallas_call(
        functools.partial(project_kernel, cap),
        out_shape=[
            jax.ShapeDtypeStruct((rows, genes), expression.dtype),
            jax.ShapeDtypeStruct((genes, width), loading.dtype),
            jax.ShapeDtypeStruct((devices * cap // 2, rows), jnp.bfloat16),
            jax.ShapeDtypeStruct((8, rows), jnp.int32),
        ]
        + [jax.ShapeDtypeStruct((rows, width), jnp.float32)] * others,
        in_specs=[HBM] * 4,
        out_specs=[VMEM] * (4 + others),
        scratch_shapes=[
            pltpu.VMEM((max(others, 1) * rows, genes), expression.dtype),
            pltpu.VMEM((2, 1, rows), jnp.int32),
            pltpu.SemaphoreType.DMA((parts + 1, CHUNKS + 1)),
        ],
        compiler_params=grant(24),
        name="project",
    )(*[pltpu.with_memory_space_constraint(operand, pltpu.HBM) for operand in operands])


def project_own_kernel(cap, x_ref, weights_ref, cluster_ref, quality_ref, rank_ref, width_ref, *refs):
    out_ref, spare_ref, pick_ref, side_ref = refs
    out_ref[...] = jnp.dot(x_ref[...], weights_ref[...], preferred_element_type=jnp.float32)
    cells = x_ref.shape[0]
    live = quality_ref[...] == 1
    widths = jnp.where(live, width_ref[...].astype(jnp.float32), 0.0)
    rank = rank_ref[:1, :]
    slot = jnp.where(live, cluster_ref[...] * cap + rank, -1)
    slot = jnp.transpose(jnp.broadcast_to(slot, (8, cells)))[:, :1]
    half = pick_ref.shape[1]
    side = jnp.where(slot < 0, -1, jnp.where(slot < half, 0, 1))
    side_ref[...] = jnp.broadcast_to(side, side_ref.shape)
    place = slot - jnp.maximum(side, 0) * half
    pick_ref[...] = jnp.where(iota(pick_ref.shape, 1) == place, 1.0, 0.0).astype(jnp.bfloat16)
    member = iota((spare_ref.shape[0], cells), 0) == cluster_ref[...]
    owned = jnp.where(member, widths, 0.0).astype(jnp.bfloat16)
    same_rank = jnp.where(lax.rem(iota((LANES, cells), 0), cap) == rank, 1.0, 0.0)
    spare_ref[...] = lax.dot_general(
        owned, same_rank.astype(jnp.bfloat16), NT, preferred_element_type=jnp.float32
    )


def project_own(own, weights, cluster, quality, rank, kernel_width, devices, cap):
    rows, genes = own.shape
    width = weights.shape[1]
    return pl.pallas_call(
        functools.partial(project_own_kernel, cap),
        out_shape=[
            jax.ShapeDtypeStruct((rows, width), jnp.float32),
            jax.ShapeDtypeStruct((devices, LANES), jnp.float32),
            jax.ShapeDtypeStruct((rows, devices * cap // 2), jnp.bfloat16),
            jax.ShapeDtypeStruct((rows, width), jnp.int32),
        ],
        in_specs=[VMEM] * 6,
        out_specs=[VMEM] * 4,
        cost_estimate=pl.CostEstimate(
            flops=2 * rows * genes * width,
            bytes_accessed=2 * genes * (rows + width),
            transcendentals=0,
        ),
        compiler_params=grant(10),
        name="project_own",
    )(
        own,
        weights,
        cluster.reshape(1, rows),
        quality.reshape(1, rows),
        rank,
        kernel_width.reshape(1, rows),
    )


def pack_kernel(place_ref, side_ref, spare_ref, *refs):
    *parts, packed_ref, embedded_ref = refs
    total = parts[0][...]
    for part in parts[1:]:
        total = total + part[...]
    embedded = total.astype(jnp.bfloat16)
    embedded_ref[...] = embedded
    side = side_ref[...]
    halves = [jnp.where(side == half, total, 0.0).astype(jnp.bfloat16) for half in range(2)]
    both = jnp.concatenate(halves, axis=1)
    rows = jnp.dot(place_ref[...], both, preferred_element_type=jnp.float32)
    n_dest, slabs, slab, width = packed_ref.shape
    for half in range(2):
        part = rows[:, half * width : (half + 1) * width].astype(jnp.bfloat16)
        part = part.reshape(n_dest // 2, slabs - 1, slab, width)
        packed_ref[half * n_dest // 2 : (half + 1) * n_dest // 2, : slabs - 1] = part
    spare = jnp.broadcast_to(spare_ref[...][:, None, None, :], (n_dest, 1, slab, width))
    packed_ref[:, slabs - 1 :] = spare.astype(jnp.bfloat16)


def pack(parts, place, side, spare, cap):
    cells, width = parts[0].shape
    return pl.pallas_call(
        pack_kernel,
        out_shape=[
            jax.ShapeDtypeStruct((spare.shape[0], cap // SLAB + 1, SLAB, width), jnp.bfloat16),
            jax.ShapeDtypeStruct((cells, width), jnp.bfloat16),
        ],
        in_specs=[VMEM] * (3 + len(parts)),
        out_specs=[VMEM] * 2,
        compiler_params=grant(10),
        name="pack",
    )(place, side, spare, *parts)


def diffuse_kernel(row_block, cap, arrived_ref, out_ref, rows, affinity, step):
    slots, width = out_ref.shape
    slabs = arrived_ref.shape[1] - 1
    groups = slots // LANES
    per = LANES // cap
    shape = (groups, LANES)
    source = lax.div(iota(shape, 1), cap)
    widths = jnp.zeros(shape, jnp.float32)
    half_norms = jnp.zeros(shape, jnp.float32)
    rows[:, :width] = arrived_ref[:, :slabs].reshape(slots, width)
    for g in range(groups):
        block = pl.ds(g * LANES, LANES)
        line = jnp.zeros(shape, jnp.float32)
        for q in range(per):
            last = arrived_ref[g * per + q, slabs].astype(jnp.float32)[:1, :]
            line = jnp.where(source == q, last, line)
        embedded = rows[block, :width]
        rows[block, width:] = jnp.ones((LANES, LANES), jnp.bfloat16)
        wide = embedded.astype(jnp.float32)
        norm = jnp.sum(jnp.transpose(wide * wide), axis=0, keepdims=True)
        here = iota(shape, 0) == g
        widths = jnp.where(here, line, widths)
        half_norms = jnp.where(here, 0.5 * norm, half_norms)
    present = widths > 0
    half_norms = jnp.where(present, half_norms, FAR)
    inverse = jnp.where(present, 1.0 / jnp.where(present, widths, 1.0), 1.0)
    norm_cols = jnp.transpose(half_norms)
    gain_cols = jnp.transpose(inverse * (2.0 * LOG2E))

    def across(lines):
        return jnp.concatenate([lines[g : g + 1, :] for g in range(groups)], axis=1)

    def down(cols, b):
        first, count = b * row_block // LANES, row_block // LANES
        return jnp.concatenate([cols[:, g : g + 1] for g in range(first, first + count)], axis=0)

    norm_row, inverse_row = across(half_norms), across(inverse)
    blocks = [pl.ds(b * row_block, row_block) for b in range(slots // row_block)]
    one_steps, scales = [], []
    for b, block in enumerate(blocks):
        first = b * row_block
        beyond = pl.ds(first, slots - first)
        products = lax.dot_general(
            rows[block, :width], rows[beyond, :width], NT, preferred_element_type=jnp.float32
        )
        power = (products - norm_row[:, first:] - down(norm_cols, b)) * (
            down(gain_cols, b) * inverse_row[:, first:]
        )
        weights = jnp.exp2(power).astype(jnp.bfloat16)
        affinity[block, beyond] = weights
        for later in range(b + 1, len(blocks)):
            start = (later - b) * row_block
            affinity[blocks[later], block] = jnp.transpose(weights[:, start : start + row_block])
        weights = affinity[block, :]
        both = jnp.dot(weights, rows[...], preferred_element_type=jnp.float32)
        total = both[:, width:]
        scale = 1.0 / jnp.where(total > 0, total, 1.0)
        one_step = 0.5 * (rows[block, :width].astype(jnp.float32) + both[:, :width] * scale)
        step[block, :] = one_step.astype(jnp.bfloat16)
        one_steps.append(one_step)
        scales.append(scale)
    tall = slots // TALL_BLOCKS
    join = len(blocks) // TALL_BLOCKS
    for t in range(TALL_BLOCKS):
        block = pl.ds(t * tall, tall)
        again = jnp.dot(affinity[block, :], step[...], preferred_element_type=jnp.float32)
        for b in range(t * join, (t + 1) * join):
            start = b * row_block - t * tall
            more = again[start : start + row_block] * scales[b]
            out_ref[blocks[b], :] = (0.5 * (one_steps[b] + more)).astype(out_ref.dtype)


def diffuse(arrived, cap):
    sources, _, _, width = arrived.shape
    slots = sources * cap
    return pl.pallas_call(
        functools.partial(diffuse_kernel, ROW_BLOCK, cap),
        out_shape=jax.ShapeDtypeStruct((slots, width), jnp.bfloat16),
        in_specs=[VMEM],
        out_specs=VMEM,
        scratch_shapes=[
            pltpu.VMEM((slots, width + LANES), jnp.bfloat16),
            pltpu.VMEM((slots, slots), jnp.bfloat16),
            pltpu.VMEM((slots, width), jnp.bfloat16),
        ],
        compiler_params=grant(16),
        name="diffuse",
    )(arrived)


def pick_kernel(pick_ref, side_ref, returned_ref, embedded_ref, out_ref, buf, sems):
    cells, width = out_ref.shape
    half = pick_ref.shape[1]
    both = jnp.concatenate([returned_ref[:half, :], returned_ref[half:, :]], axis=1)
    depth = cells // PICK_CHUNKS
    copies = []
    for k in range(PICK_CHUNKS):
        block = pl.ds(k * depth, depth)
        picked = jnp.dot(pick_ref[block, :], both, preferred_element_type=jnp.float32)
        side = side_ref[block, :]
        kept = embedded_ref[block, :].astype(jnp.float32)
        second = jnp.where(side == 1, picked[:, width:], kept)
        buf[block, :] = jnp.where(side == 0, picked[:, :width], second)
        copies.append(pltpu.make_async_copy(buf.at[block, :], out_ref.at[block, :], sems.at[k]))
        copies[k].start()
    for copy in copies:
        copy.wait()


def pick(pick_onehot, side, returned, embedded):
    cells, width = embedded.shape
    return pl.pallas_call(
        pick_kernel,
        out_shape=jax.ShapeDtypeStruct((cells, width), jnp.float32),
        in_specs=[VMEM] * 4,
        out_specs=HBM,
        scratch_shapes=[
            pltpu.VMEM((cells, width), jnp.float32),
            pltpu.SemaphoreType.DMA((PICK_CHUNKS,)),
        ],
        compiler_params=grant(8),
        name="pick",
    )(pick_onehot, side, returned, embedded)


def body(expression, loading, kernel_width, cluster, quality):
    gene_count = lax.axis_size("genes")
    devices = gene_count * lax.axis_size("cells")
    cap = SLAB * pl.cdiv(max(1, 2 * kernel_width.shape[0] // devices), SLAB)
    width = loading.shape[1]
    own, weights, place, rank, *partials = project(
        expression, loading, cluster, quality, gene_count, devices, cap
    )
    parts = []
    for shift, partial in enumerate(partials, 1):
        ring = [(i, (i + shift) % gene_count) for i in range(gene_count)]
        parts.append(lax.ppermute(partial, "genes", ring))
    own_part, spare, pick_onehot, side = project_own(
        own, weights, cluster, quality, rank, kernel_width, devices, cap
    )
    parts.append(own_part)
    packed, embedded = pack(parts, place, side, spare, cap)
    arrived = lax.all_to_all(packed, AXES, split_axis=0, concat_axis=0, tiled=True)
    smoothed = diffuse(arrived, cap)
    returned = lax.all_to_all(
        smoothed.reshape(devices, cap, width), AXES, split_axis=0, concat_axis=0, tiled=True
    )
    return pick(pick_onehot, side, returned.reshape(devices * cap, width), embedded)


def solution(mesh):
    return jax.shard_map(
        body,
        mesh=mesh,
        in_specs=(
            P("cells", "genes"),
            P("genes", None),
            P(AXES),
            P(AXES, None),
            P(AXES),
        ),
        out_specs=P(AXES, None),
        check_vma=False,
    )
```

```python
import functools

import jax
import jax.numpy as jnp
from jax import lax
from jax.experimental import pallas as pl
from jax.experimental.pallas import tpu as pltpu
from jax.sharding import PartitionSpec as P

AXES = ("cells", "genes")
LANES = 128
LOG2E = 1.4426950408889634
FAR = 1e30
NT = (((1,), (1,)), ((), ()))
VMEM = pl.BlockSpec(memory_space=pltpu.VMEM)
HBM = pl.BlockSpec(memory_space=pltpu.HBM)
CHUNKS = 2
ROW_BLOCK = 256
TALL_BLOCKS = 2
PICK_CHUNKS = 4
SLAB = 2


def grant(mebibytes):
    return pltpu.CompilerParams(
        vmem_limit_bytes=mebibytes << 20,
    )


def iota(shape, axis):
    return lax.broadcasted_iota(jnp.int32, shape, axis)


def ranks(cluster_row, live, clusters):
    cells = cluster_row.shape[1]
    member = jnp.where((iota((clusters, cells), 0) == cluster_row) & live, 1.0, 0.0)
    earlier = jnp.where(iota((cells, cells), 0) < iota((cells, cells), 1), 1.0, 0.0)
    before = jnp.dot(
        member.astype(jnp.bfloat16),
        earlier.astype(jnp.bfloat16),
        preferred_element_type=jnp.float32,
    )
    return jnp.sum(before * member, axis=0, keepdims=True).astype(jnp.int32)


def project_kernel(cap, x_ref, loading_ref, cluster_ref, quality_ref, *refs):
    own_ref, weights_ref, place_ref, rank_ref, *out_refs, x_buf, labels, sems = refs
    parts = len(out_refs) + 1
    rows = own_ref.shape[0]
    depth = rows // CHUNKS
    me = lax.axis_index("genes")
    small = [
        pltpu.make_async_copy(cluster_ref, labels.at[0], sems.at[0, CHUNKS]),
        pltpu.make_async_copy(quality_ref, labels.at[1], sems.at[1, CHUNKS]),
    ]
    weights = pltpu.make_async_copy(loading_ref, weights_ref, sems.at[parts, CHUNKS])
    for copy in [*small, weights]:
        copy.start()
    copies = []
    for p in range(parts):
        buffer = own_ref if p == parts - 1 else x_buf.at[pl.ds(p * rows, rows), :]
        first = lax.rem(me + p + 1, parts) * rows
        copies.append([])
        for c in range(CHUNKS):
            source = x_ref.at[pl.ds(pl.multiple_of(first + c * depth, depth), depth), :]
            target = buffer.at[pl.ds(c * depth, depth), :]
            copies[p].append(pltpu.make_async_copy(source, target, sems.at[p, c]))
            copies[p][c].start()
    for copy in small:
        copy.wait()
    cluster_row = labels[0]
    live = labels[1] == 1
    half = place_ref.shape[0]
    rank = ranks(cluster_row, live, 2 * half // cap)
    rank_ref[...] = jnp.broadcast_to(rank, rank_ref.shape)
    place = jnp.where(live, lax.rem(cluster_row * cap + rank, half), -1)
    place_ref[...] = jnp.where(iota(place_ref.shape, 0) == place, 1.0, 0.0).astype(jnp.bfloat16)
    weights.wait()
    for p in range(parts):
        for c, copy in enumerate(copies[p]):
            copy.wait()
            if p < parts - 1:
                out_refs[p][pl.ds(c * depth, depth), :] = jnp.dot(
                    x_buf[pl.ds(p * rows + c * depth, depth), :],
                    weights_ref[...],
                    preferred_element_type=jnp.float32,
                )


def project(expression, loading, cluster, quality, parts, devices, cap):
    cells, genes = expression.shape
    width = loading.shape[1]
    rows = cells // parts
    others = parts - 1
    operands = (expression, loading, cluster.reshape(1, rows), quality.reshape(1, rows))
    return pl.pallas_call(
        functools.partial(project_kernel, cap),
        out_shape=[
            jax.ShapeDtypeStruct((rows, genes), expression.dtype),
            jax.ShapeDtypeStruct((genes, width), loading.dtype),
            jax.ShapeDtypeStruct((devices * cap // 2, rows), jnp.bfloat16),
            jax.ShapeDtypeStruct((8, rows), jnp.int32),
        ]
        + [jax.ShapeDtypeStruct((rows, width), jnp.float32)] * others,
        in_specs=[HBM] * 4,
        out_specs=[VMEM] * (4 + others),
        scratch_shapes=[
            pltpu.VMEM((max(others, 1) * rows, genes), expression.dtype),
            pltpu.VMEM((2, 1, rows), jnp.int32),
            pltpu.SemaphoreType.DMA((parts + 1, CHUNKS + 1)),
        ],
        compiler_params=grant(24),
        name="project",
    )(*[pltpu.with_memory_space_constraint(operand, pltpu.HBM) for operand in operands])


def project_own_kernel(cap, x_ref, weights_ref, cluster_ref, quality_ref, rank_ref, width_ref, *refs):
    out_ref, spare_ref, pick_ref, side_ref = refs
    out_ref[...] = jnp.dot(x_ref[...], weights_ref[...], preferred_element_type=jnp.float32)
    cells = x_ref.shape[0]
    live = quality_ref[...] == 1
    widths = jnp.where(live, width_ref[...].astype(jnp.float32), 0.0)
    rank = rank_ref[:1, :]
    slot = jnp.where(live, cluster_ref[...] * cap + rank, -1)
    slot = jnp.transpose(jnp.broadcast_to(slot, (8, cells)))[:, :1]
    half = pick_ref.shape[1]
    side = jnp.where(slot < 0, -1, jnp.where(slot < half, 0, 1))
    side_ref[...] = jnp.broadcast_to(side, side_ref.shape)
    place = slot - jnp.maximum(side, 0) * half
    pick_ref[...] = jnp.where(iota(pick_ref.shape, 1) == place, 1.0, 0.0).astype(jnp.bfloat16)
    member = iota((spare_ref.shape[0], cells), 0) == cluster_ref[...]
    owned = jnp.where(member, widths, 0.0).astype(jnp.bfloat16)
    same_rank = jnp.where(lax.rem(iota((LANES, cells), 0), cap) == rank, 1.0, 0.0)
    spare_ref[...] = lax.dot_general(
        owned, same_rank.astype(jnp.bfloat16), NT, preferred_element_type=jnp.float32
    )


def project_own(own, weights, cluster, quality, rank, kernel_width, devices, cap):
    rows, genes = own.shape
    width = weights.shape[1]
    return pl.pallas_call(
        functools.partial(project_own_kernel, cap),
        out_shape=[
            jax.ShapeDtypeStruct((rows, width), jnp.float32),
            jax.ShapeDtypeStruct((devices, LANES), jnp.float32),
            jax.ShapeDtypeStruct((rows, devices * cap // 2), jnp.bfloat16),
            jax.ShapeDtypeStruct((rows, width), jnp.int32),
        ],
        in_specs=[VMEM] * 6,
        out_specs=[VMEM] * 4,
        cost_estimate=pl.CostEstimate(
            flops=2 * rows * genes * width,
            bytes_accessed=2 * genes * (rows + width),
            transcendentals=0,
        ),
        compiler_params=grant(10),
        name="project_own",
    )(
        own,
        weights,
        cluster.reshape(1, rows),
        quality.reshape(1, rows),
        rank,
        kernel_width.reshape(1, rows),
    )


def pack_kernel(place_ref, side_ref, spare_ref, *refs):
    *parts, packed_ref, embedded_ref = refs
    total = parts[0][...]
    for part in parts[1:]:
        total = total + part[...]
    embedded = total.astype(jnp.bfloat16)
    embedded_ref[...] = embedded
    side = side_ref[...]
    halves = [jnp.where(side == half, total, 0.0).astype(jnp.bfloat16) for half in range(2)]
    both = jnp.concatenate(halves, axis=1)
    rows = jnp.dot(place_ref[...], both, preferred_element_type=jnp.float32)
    n_dest, slabs, slab, width = packed_ref.shape
    for half in range(2):
        part = rows[:, half * width : (half + 1) * width].astype(jnp.bfloat16)
        part = part.reshape(n_dest // 2, slabs - 1, slab, width)
        packed_ref[half * n_dest // 2 : (half + 1) * n_dest // 2, : slabs - 1] = part
    spare = jnp.broadcast_to(spare_ref[...][:, None, None, :], (n_dest, 1, slab, width))
    packed_ref[:, slabs - 1 :] = spare.astype(jnp.bfloat16)


def pack(parts, place, side, spare, cap):
    cells, width = parts[0].shape
    return pl.pallas_call(
        pack_kernel,
        out_shape=[
            jax.ShapeDtypeStruct((spare.shape[0], cap // SLAB + 1, SLAB, width), jnp.bfloat16),
            jax.ShapeDtypeStruct((cells, width), jnp.bfloat16),
        ],
        in_specs=[VMEM] * (3 + len(parts)),
        out_specs=[VMEM] * 2,
        compiler_params=grant(10),
        name="pack",
    )(place, side, spare, *parts)


def diffuse_kernel(row_block, cap, arrived_ref, out_ref, rows, affinity, step):
    slots, width = out_ref.shape
    slabs = arrived_ref.shape[1] - 1
    groups = slots // LANES
    per = LANES // cap
    shape = (groups, LANES)
    source = lax.div(iota(shape, 1), cap)
    widths = jnp.zeros(shape, jnp.float32)
    half_norms = jnp.zeros(shape, jnp.float32)
    rows[:, :width] = arrived_ref[:, :slabs].reshape(slots, width)
    for g in range(groups):
        block = pl.ds(g * LANES, LANES)
        line = jnp.zeros(shape, jnp.float32)
        for q in range(per):
            last = arrived_ref[g * per + q, slabs].astype(jnp.float32)[:1, :]
            line = jnp.where(source == q, last, line)
        embedded = rows[block, :width]
        rows[block, width:] = jnp.ones((LANES, LANES), jnp.bfloat16)
        wide = embedded.astype(jnp.float32)
        norm = jnp.sum(jnp.transpose(wide * wide), axis=0, keepdims=True)
        here = iota(shape, 0) == g
        widths = jnp.where(here, line, widths)
        half_norms = jnp.where(here, 0.5 * norm, half_norms)
    present = widths > 0
    half_norms = jnp.where(present, half_norms, FAR)
    inverse = jnp.where(present, 1.0 / jnp.where(present, widths, 1.0), 1.0)
    norm_cols = jnp.transpose(half_norms)
    gain_cols = jnp.transpose(inverse * (2.0 * LOG2E))

    def across(lines):
        return jnp.concatenate([lines[g : g + 1, :] for g in range(groups)], axis=1)

    def down(cols, b):
        first, count = b * row_block // LANES, row_block // LANES
        return jnp.concatenate([cols[:, g : g + 1] for g in range(first, first + count)], axis=0)

    norm_row, inverse_row = across(half_norms), across(inverse)
    blocks = [pl.ds(b * row_block, row_block) for b in range(slots // row_block)]
    one_steps, scales = [], []
    for b, block in enumerate(blocks):
        first = b * row_block
        beyond = pl.ds(first, slots - first)
        products = lax.dot_general(
            rows[block, :width], rows[beyond, :width], NT, preferred_element_type=jnp.float32
        )
        power = (products - norm_row[:, first:] - down(norm_cols, b)) * (
            down(gain_cols, b) * inverse_row[:, first:]
        )
        weights = jnp.exp2(power).astype(jnp.bfloat16)
        affinity[block, beyond] = weights
        for later in range(b + 1, len(blocks)):
            start = (later - b) * row_block
            affinity[blocks[later], block] = jnp.transpose(weights[:, start : start + row_block])
        weights = affinity[block, :]
        both = jnp.dot(weights, rows[...], preferred_element_type=jnp.float32)
        total = both[:, width:]
        scale = 1.0 / jnp.where(total > 0, total, 1.0)
        one_step = 0.5 * (rows[block, :width].astype(jnp.float32) + both[:, :width] * scale)
        step[block, :] = one_step.astype(jnp.bfloat16)
        one_steps.append(one_step)
        scales.append(scale)
    tall = slots // TALL_BLOCKS
    join = len(blocks) // TALL_BLOCKS
    for t in range(TALL_BLOCKS):
        block = pl.ds(t * tall, tall)
        again = jnp.dot(affinity[block, :], step[...], preferred_element_type=jnp.float32)
        for b in range(t * join, (t + 1) * join):
            start = b * row_block - t * tall
            more = again[start : start + row_block] * scales[b]
            out_ref[blocks[b], :] = (0.5 * (one_steps[b] + more)).astype(out_ref.dtype)


def diffuse(arrived, cap):
    sources, _, _, width = arrived.shape
    slots = sources * cap
    return pl.pallas_call(
        functools.partial(diffuse_kernel, ROW_BLOCK, cap),
        out_shape=jax.ShapeDtypeStruct((slots, width), jnp.bfloat16),
        in_specs=[VMEM],
        out_specs=VMEM,
        scratch_shapes=[
            pltpu.VMEM((slots, width + LANES), jnp.bfloat16),
            pltpu.VMEM((slots, slots), jnp.bfloat16),
            pltpu.VMEM((slots, width), jnp.bfloat16),
        ],
        compiler_params=grant(16),
        name="diffuse",
    )(arrived)


def pick_kernel(pick_ref, side_ref, returned_ref, embedded_ref, out_ref, buf, sems):
    cells, width = out_ref.shape
    half = pick_ref.shape[1]
    both = jnp.concatenate([returned_ref[:half, :], returned_ref[half:, :]], axis=1)
    depth = cells // PICK_CHUNKS
    copies = []
    for k in range(PICK_CHUNKS):
        block = pl.ds(k * depth, depth)
        picked = jnp.dot(pick_ref[block, :], both, preferred_element_type=jnp.float32)
        side = side_ref[block, :]
        kept = embedded_ref[block, :].astype(jnp.float32)
        second = jnp.where(side == 1, picked[:, width:], kept)
        buf[block, :] = jnp.where(side == 0, picked[:, :width], second)
        copies.append(pltpu.make_async_copy(buf.at[block, :], out_ref.at[block, :], sems.at[k]))
        copies[k].start()
    for copy in copies:
        copy.wait()


def pick(pick_onehot, side, returned, embedded):
    cells, width = embedded.shape
    return pl.pallas_call(
        pick_kernel,
        out_shape=jax.ShapeDtypeStruct((cells, width), jnp.float32),
        in_specs=[VMEM] * 4,
        out_specs=HBM,
        scratch_shapes=[
            pltpu.VMEM((cells, width), jnp.float32),
            pltpu.SemaphoreType.DMA((PICK_CHUNKS,)),
        ],
        compiler_params=grant(8),
        name="pick",
    )(pick_onehot, side, returned, embedded)


def body(expression, loading, kernel_width, cluster, quality):
    gene_count = lax.axis_size("genes")
    devices = gene_count * lax.axis_size("cells")
    cap = SLAB * pl.cdiv(max(1, 2 * kernel_width.shape[0] // devices), SLAB)
    width = loading.shape[1]
    own, weights, place, rank, *partials = project(
        expression, loading, cluster, quality, gene_count, devices, cap
    )
    parts = []
    for shift, partial in enumerate(partials, 1):
        ring = [(i, (i + shift) % gene_count) for i in range(gene_count)]
        parts.append(lax.ppermute(partial, "genes", ring))
    own_part, spare, pick_onehot, side = project_own(
        own, weights, cluster, quality, rank, kernel_width, devices, cap
    )
    parts.append(own_part)
    packed, embedded = pack(parts, place, side, spare, cap)
    arrived = lax.all_to_all(packed, AXES, split_axis=0, concat_axis=0, tiled=True)
    smoothed = diffuse(arrived, cap)
    returned = lax.all_to_all(
        smoothed, AXES, split_axis=0, concat_axis=0, tiled=True
    )
    return pick(pick_onehot, side, returned.reshape(devices * cap, width), embedded)


def solution(mesh):
    return jax.shard_map(
        body,
        mesh=mesh,
        in_specs=(
            P("cells", "genes"),
            P("genes", None),
            P(AXES),
            P(AXES, None),
            P(AXES),
        ),
        out_specs=P(AXES, None),
        check_vma=False,
    )
```
